32 devices in a mesh: gene: 8 (over z, x), cell: 4 (over y, core).
Axes of the slice: x: 2, y: 2, z: 4, core: 2. Of those that a mesh axis runs over, the one named last changes fastest.
Arguments:
- gene_tokens: bfloat16 [16, 4096, 768], P('cell', 'gene')
- latents: bfloat16 [64, 768], replicated, may hold values from -6 to 6
- head_temp: float32 [12], replicated, may hold values from 1.5 to 4
- w_key: bfloat16 [768, 768], replicated, may hold values from -0.21875 to 0.21875
- w_value: bfloat16 [768, 768], replicated, may hold values from -0.21875 to 0.21875
- w_out: bfloat16 [768, 768], replicated, may hold values from -0.21875 to 0.21875
- w_set_qkv: bfloat16 [768, 2304], replicated, may hold values from -0.21875 to 0.21875
- w_set_out: bfloat16 [768, 768], replicated, may hold values from -0.21875 to 0.21875
- set_ids: int32 [16], P('cell'), may hold values from 0 to 7, as said below
Outputs:
- latent_states: bfloat16 [16, 64, 768], P('cell', 'gene')
- set_states: bfloat16 [16, 768], P('cell')
The draws below stay inside these ranges and needn't reach their ends.
Inputs may be any that keep to these rules, and one draw needn't show every extreme that they name: `set_ids`: set s is held by index s mod 4 of cell. At most 2 cells of one device's block belong to sets held by one index, and in every draw one index holds the sets of exactly 2 cells of every device's block.
All inputs are finite; a program needn't handle non-finite values.
Results may differ from the reference program's by a relative error of at most 0.012.
Values may be sent and summed in bfloat16 or wider, within the bound.
A program may use at most 64 MiB of HBM per device.

```python
import math
import jax
import jax.numpy as jnp
from jax import lax

D = 768
H = 12
LAT = 64
CELL_DEV = 4
SPG = 2
CAP = 2
GENES = 4096
CELLS = 16
N_CELL = 4


def draw_gene_tokens(key, part):
    first = jax.random.fold_in(key, 0)
    tokens = jax.random.normal(first, (CELLS, GENES, D), jnp.float32)
    return tokens.astype(jnp.bfloat16)


def draw_set_ids(key, part):
    first, second, third, fourth = jax.random.split(key, 4)
    heavy = jax.random.randint(first, (), 0, N_CELL)
    column = jnp.arange(CELL_DEV)[None, :]
    others = (heavy + 1 + jax.random.randint(second, (N_CELL, CELL_DEV), 0, N_CELL - 1)) % N_CELL
    owners = jnp.where(column < CAP, heavy, others)
    picks = jax.random.randint(third, (N_CELL, CELL_DEV), 0, SPG)
    labels = (owners + N_CELL * picks).astype(jnp.int32)
    row_keys = jax.random.split(fourth, N_CELL)
    shuffled = jax.vmap(lambda row_key, row: jax.random.permutation(row_key, row))(row_keys, labels)
    return shuffled.reshape(CELLS).astype(jnp.int32)


def noise(rng, extent, deviation, bound, held_as=jnp.bfloat16):
    return jnp.clip(deviation * jax.random.normal(rng, extent, jnp.float32), -bound, bound).astype(held_as)


def setup_inputs(seed: int = 0) -> dict:
    key_list = jax.random.split(jax.random.key(seed), 10)
    gene_tokens = draw_gene_tokens(jax.random.fold_in(key_list[9], 71), 0)
    latents = noise(key_list[1], (LAT, D), 1.0, 6.0)
    head_temp = jnp.clip(jnp.exp(jax.random.uniform(key_list[2], (H,), jnp.float32, math.log(1.5), math.log(4.0))), 1.5, 4.0)
    w_key = noise(key_list[3], (D, D), D ** -0.5, 0.21875)
    w_value = noise(key_list[4], (D, D), D ** -0.5, 0.21875)
    w_out = noise(key_list[5], (D, D), D ** -0.5, 0.21875)
    w_set_qkv = noise(key_list[6], (D, 3 * D), D ** -0.5, 0.21875)
    w_set_out = noise(key_list[7], (D, D), D ** -0.5, 0.21875)
    set_ids = draw_set_ids(jax.random.fold_in(key_list[9], 71), 0)
    return {"gene_tokens": gene_tokens, "latents": latents, "head_temp": head_temp, "w_key": w_key, "w_value": w_value, "w_out": w_out, "w_set_qkv": w_set_qkv, "w_set_out": w_set_out, "set_ids": set_ids}


EPSILON = 1e-06

def to_wide(array):
    return lax.optimization_barrier(array).astype(jnp.float32)

def head_norm(array, head_count):
    shaped = array.reshape(array.shape[:-1] + (head_count, array.shape[-1] // head_count))
    return shaped * lax.rsqrt(lax.optimization_barrier(jnp.mean(shaped * shaped, axis=-1, keepdims=True)) + EPSILON)

def set_project(inputs, w_set_qkv, head_count):
    model_width = inputs.shape[1]
    head_size = model_width // head_count
    projected = jnp.dot(inputs, w_set_qkv, preferred_element_type=jnp.float32)
    queries = (head_norm(projected[:, :model_width], head_count) / math.sqrt(head_size)).astype(jnp.bfloat16)
    key_rows = head_norm(projected[:, model_width:2 * model_width], head_count).astype(jnp.bfloat16)
    value_rows = projected[:, 2 * model_width:].reshape(inputs.shape[0], head_count, head_size).astype(jnp.bfloat16)
    return (queries, key_rows, value_rows)

def set_attend(queries, key_rows, value_rows, query_ids, key_ids, residual, w_set_out):
    scores = jnp.einsum('qhe,khe->hqk', to_wide(queries), to_wide(key_rows))
    matching = query_ids[:, None] == key_ids[None, :]
    weights = jnp.where(matching[None], jnp.exp(scores), 0.0)
    totals = lax.optimization_barrier(jnp.sum(weights, axis=2))
    numerator = jnp.einsum('hqk,khe->qhe', to_wide(weights.astype(jnp.bfloat16)), to_wide(value_rows))
    attended = (numerator / jnp.transpose(totals)[:, :, None]).reshape(queries.shape[0], -1).astype(jnp.bfloat16)
    return (to_wide(residual) + jnp.dot(attended, w_set_out, preferred_element_type=jnp.float32)).astype(jnp.bfloat16)

def reference(gene_tokens, latents, head_temp, w_key, w_value, w_out, w_set_qkv, w_set_out, set_ids):
    head_count = head_temp.shape[0]
    head_size = D // head_count
    queries = (head_norm(latents.astype(jnp.float32), head_count) * (head_temp[:, None] / math.sqrt(head_size))).astype(jnp.bfloat16)

    def one_cell(tokens):
        key_rows = head_norm(jnp.dot(tokens, w_key, preferred_element_type=jnp.float32), head_count).astype(jnp.bfloat16)
        value_rows = jnp.dot(tokens, w_value, preferred_element_type=jnp.float32).astype(jnp.bfloat16)
        value_rows = value_rows.reshape(tokens.shape[0], head_count, head_size)
        scores = jnp.einsum('lhe,ghe->hlg', to_wide(queries), to_wide(key_rows))
        weights = jnp.exp(scores)
        totals = lax.optimization_barrier(jnp.sum(weights, axis=2))
        numerator = jnp.einsum('hlg,ghe->lhe', to_wide(weights.astype(jnp.bfloat16)), to_wide(value_rows))
        attended = (numerator / jnp.transpose(totals)[:, :, None]).reshape(latents.shape[0], D).astype(jnp.bfloat16)
        return latents.astype(jnp.float32) + jnp.dot(attended, w_out, preferred_element_type=jnp.float32)
    mixed_rows = lax.map(one_cell, gene_tokens)
    latent_states = mixed_rows.astype(jnp.bfloat16)
    pooled = lax.optimization_barrier(jnp.mean(mixed_rows, axis=1))
    set_input = (pooled * lax.rsqrt(lax.optimization_barrier(jnp.mean(pooled * pooled, axis=1, keepdims=True)) + EPSILON)).astype(jnp.bfloat16)
    set_queries, set_keys, set_values = set_project(set_input, w_set_qkv, head_count)
    set_states = set_attend(set_queries, set_keys, set_values, set_ids, set_ids, set_input, w_set_out)
    return (latent_states, set_states)
```

```python
import functools
import math

import jax
import jax.numpy as jnp
from jax import lax
from jax.experimental import pallas as pl
from jax.experimental.pallas import tpu as pltpu
from jax.sharding import PartitionSpec as P

EPSILON = 1e-06
MESH = pl.DeviceIdType.MESH
F32, BF16 = jnp.float32, jnp.bfloat16
HEAD = 64
LANES = 128
GROUP = 256
ROWS = 8


def iota(shape, dim):
    return lax.broadcasted_iota(jnp.int32, shape, dim)


def dot(a, b):
    return jnp.dot(a, b, preferred_element_type=F32)


def dot_nt(a, b):
    return lax.dot_general(a, b, (((1,), (1,)), ((), ())), preferred_element_type=F32)


def dot_split(a, b):
    high = a.astype(BF16)
    low = (a - high.astype(F32)).astype(BF16)
    return dot(high, b) + dot(low, b)


def kernel(
    n,
    m,
    tok_hbm,
    lat_hbm,
    temp_ref,
    wk_hbm,
    wv_hbm,
    wo_hbm,
    wqkv_hbm,
    wso_hbm,
    ids_ref,
    lat_out,
    set_out,
    tok,
    lat,
    wk,
    wv,
    wo,
    wqkv,
    wso,
    qb,
    send,
    recv,
    acc,
    psum,
    psend,
    precv,
    ssend,
    srecv,
    in_sem,
    tok_sem,
    send_sem,
    recv_sem,
    late_sem,
):
    cells, genes, width = tok.shape
    latents = lat.shape[0]
    portion = latents // n
    heads = width // HEAD
    groups = width // GROUP
    per_group = GROUP // HEAD
    half = width // 2
    gene = lax.axis_index("gene")
    cell = lax.axis_index("cell")

    barrier = pltpu.get_barrier_semaphore()
    for o in range(1, n):
        pl.semaphore_signal(
            barrier, inc=1, device_id=(lax.rem(gene + o, n), cell), device_id_type=MESH
        )
    for o in range(1, m):
        pl.semaphore_signal(
            barrier, inc=1, device_id=(gene, lax.rem(cell + o, m)), device_id_type=MESH
        )

    lat_in = pltpu.make_async_copy(lat_hbm, lat, in_sem.at[0])
    wk_in = pltpu.make_async_copy(wk_hbm, wk, in_sem.at[1])
    wv_in = pltpu.make_async_copy(wv_hbm, wv, in_sem.at[2])
    wo_in = pltpu.make_async_copy(wo_hbm, wo, in_sem.at[3])
    wqkv_in = pltpu.make_async_copy(wqkv_hbm, wqkv, in_sem.at[4])
    wso_in = pltpu.make_async_copy(wso_hbm, wso, in_sem.at[5])

    def tok_in(c):
        return pltpu.make_async_copy(tok_hbm.at[c], tok.at[c], tok_sem.at[c])

    lat_in.start()
    wk_in.start()
    tok_in(0).start()
    wv_in.start()
    for c in range(1, cells):
        tok_in(c).start()
    wo_in.start()
    wqkv_in.start()
    wso_in.start()

    same_head = (iota((GROUP, GROUP), 0) >> 6) == (iota((GROUP, GROUP), 1) >> 6)
    mean_head = jnp.where(same_head, 1.0 / HEAD, 0.0).astype(BF16)
    col_head = iota((latents, GROUP), 1) >> 6
    lane = iota((latents, LANES), 1)

    def head_scale(x):
        return lax.rsqrt(dot((x * x).astype(BF16), mean_head) + EPSILON)

    lat_in.wait()
    for i in range(groups):
        block = lat[:, i * GROUP : (i + 1) * GROUP].astype(F32)
        mean_square = dot_split(block * block, mean_head)
        temp = jnp.zeros((latents, GROUP), F32)
        for h in range(per_group):
            temp = jnp.where(
                col_head == h, temp_ref[i * per_group + h] / math.sqrt(HEAD), temp
            )
        query = block * lax.rsqrt(mean_square + EPSILON) * temp
        stacked = jnp.concatenate([query] * per_group, axis=0)
        qb[i] = jnp.where(same_head, stacked, 0.0).astype(BF16)

    wk_in.wait()
    wv_in.wait()
    pl.semaphore_wait(barrier, n - 1 + m - 1)

    def one_cell(c, carry):
        tok_in(c).wait()
        tokens = tok[c]
        totals = jnp.zeros((latents, LANES), F32)
        for i in range(groups):
            cols = slice(i * GROUP, (i + 1) * GROUP)
            key = dot(tokens, wk[:, cols])
            key = (key * head_scale(key)).astype(BF16)
            weights = jnp.exp(dot_nt(qb[i], key))
            value = dot(tokens, wv[:, cols]).astype(BF16)
            mixed = dot(weights.astype(BF16), value)
            total = jnp.sum(weights, axis=1, keepdims=True)
            numerator = mixed[:latents]
            for h in range(per_group):
                rows = slice(h * latents, (h + 1) * latents)
                numerator = jnp.where(col_head == h, mixed[rows], numerator)
                totals = jnp.where(lane == i * per_group + h, total[rows], totals)
            for j in range(n):
                send[c, j, :, cols] = numerator[j * portion : (j + 1) * portion].astype(BF16)
        for j in range(n):
            send[c, j, :, width:] = totals[j * portion : (j + 1) * portion].astype(BF16)
        for o in range(1, n):
            peer = lax.rem(gene + o, n)
            pltpu.make_async_remote_copy(
                src_ref=send.at[c, peer],
                dst_ref=recv.at[c, o],
                send_sem=send_sem.at[c],
                recv_sem=recv_sem.at[c],
                device_id=(peer, cell),
                device_id_type=MESH,
            ).start()
        return carry

    lax.fori_loop(0, cells, one_cell, 0)

    select = iota((cells * portion, latents), 0)
    select = lax.rem(select, portion) + gene * portion == iota((cells * portion, latents), 1)
    own_latents = dot(select.astype(F32).astype(BF16), lat[...])
    mean_latents = jnp.sum(lat[...].astype(F32), axis=0, keepdims=True) * (1.0 / latents)
    expand = iota((LANES, width), 0) == (iota((LANES, width), 1) >> 6)
    expand = expand.astype(F32).astype(BF16)
    one_hot = jnp.zeros((ROWS, LANES), F32)
    row8, lane8 = iota((ROWS, LANES), 0), iota((ROWS, LANES), 1)
    for c in range(cells):
        one_hot = jnp.where((row8 == c) & (lane8 == ids_ref[c]), 1.0, one_hot)

    for c in range(cells):
        arrived = pltpu.make_async_remote_copy(
            src_ref=send.at[c, pl.ds(0, n - 1)],
            dst_ref=recv.at[c, pl.ds(1, n - 1)],
            send_sem=send_sem.at[c],
            recv_sem=recv_sem.at[c],
            device_id=(gene, cell),
            device_id_type=MESH,
        )
        arrived.wait_recv()
        total = send[c, gene].astype(F32)
        for o in range(1, n):
            total = total + recv[c, o].astype(F32)
        acc[c * portion : (c + 1) * portion, :] = total
        arrived.wait_send()
    totals = acc[:, width:]
    is_head = iota(totals.shape, 1) < heads
    inverse = jnp.where(is_head, 1.0 / jnp.where(is_head, totals, 1.0), 0.0)
    attended = (acc[:, :width] * dot_split(inverse, expand)).astype(BF16)
    wide = attended.astype(F32)
    for c in range(cells):
        row = jnp.sum(wide[c * portion : (c + 1) * portion], axis=0, keepdims=True)
        psum[c : c + 1, :] = row[:, :half]
        psum[cells + c : cells + c + 1, :] = row[:, half:]
    psend[...] = psum[...].astype(BF16)
    for o in range(1, n):
        pltpu.make_async_remote_copy(
            src_ref=psend,
            dst_ref=precv.at[o],
            send_sem=late_sem.at[0],
            recv_sem=late_sem.at[1],
            device_id=(lax.rem(gene + o, n), cell),
            device_id_type=MESH,
        ).start()

    wo_in.wait()
    mixed_rows = own_latents + dot(attended, wo[...])
    for c in range(cells):
        lat_out[c] = mixed_rows[c * portion : (c + 1) * portion].astype(BF16)

    wqkv_in.wait()
    wso_in.wait()
    arrived = pltpu.make_async_remote_copy(
        src_ref=precv.at[pl.ds(1, n - 1)],
        dst_ref=precv.at[pl.ds(1, n - 1)],
        send_sem=late_sem.at[0],
        recv_sem=late_sem.at[1],
        device_id=(gene, cell),
        device_id_type=MESH,
    )
    arrived.wait_recv()
    summed = psend[...].astype(F32)
    for o in range(1, n):
        summed = summed + precv[o].astype(F32)
    arrived.wait_send()
    summed = jnp.concatenate([summed, pltpu.roll(summed, ROWS - cells, 0)], axis=1)
    pooled = mean_latents + dot_split(summed * (1.0 / latents), wo[...])
    scale = lax.rsqrt(jnp.mean(pooled * pooled, axis=1, keepdims=True) + EPSILON)
    own_input = (pooled * scale).astype(BF16)
    ssend[:, :width] = own_input.astype(F32)
    ssend[:, width:] = one_hot
    for o in range(1, m):
        pltpu.make_async_remote_copy(
            src_ref=ssend,
            dst_ref=srecv.at[o],
            send_sem=late_sem.at[2],
            recv_sem=late_sem.at[3],
            device_id=(gene, lax.rem(cell + o, m)),
            device_id_type=MESH,
        ).start()

    def head_rows(x):
        parts = []
        for i in range(groups):
            part = x[:, i * GROUP : (i + 1) * GROUP]
            parts.append(part * head_scale(part))
        return jnp.concatenate(parts, axis=1)

    stack = (heads * ROWS, width)
    own_head = (iota(stack, 0) >> 3) == (iota(stack, 1) >> 6)
    queries = head_rows(dot(own_input, wqkv[:, :width])) * (1.0 / math.sqrt(HEAD))
    queries = jnp.concatenate([queries] * heads, axis=0)
    queries = jnp.where(own_head, queries, 0.0).astype(BF16)
    query_sets = jnp.concatenate([one_hot] * heads, axis=0).astype(BF16)

    arrived = pltpu.make_async_remote_copy(
        src_ref=srecv.at[pl.ds(1, m - 1)],
        dst_ref=srecv.at[pl.ds(1, m - 1)],
        send_sem=late_sem.at[2],
        recv_sem=late_sem.at[3],
        device_id=(gene, cell),
        device_id_type=MESH,
    )
    arrived.wait_recv()
    every = jnp.concatenate([ssend[...]] + [srecv[o] for o in range(1, m)], axis=0).astype(BF16)
    arrived.wait_send()
    every_input, key_sets = every[:, :width], every[:, width:]
    keys_values = dot(every_input, wqkv[:, width:])
    keys = head_rows(keys_values[:, :width]).astype(BF16)
    values = keys_values[:, width:].astype(BF16)
    matching = dot_nt(query_sets, key_sets) > 0.5
    weights = jnp.where(matching, jnp.exp(dot_nt(queries, keys)), 0.0)
    total = jnp.sum(weights, axis=1, keepdims=True)
    total = jnp.where(total > 0.0, total, 1.0)
    mixed = jnp.where(own_head, dot(weights.astype(BF16), values) / total, 0.0)
    set_attended = mixed[:ROWS]
    for h in range(1, heads):
        set_attended = set_attended + mixed[h * ROWS : (h + 1) * ROWS]
    states = own_input.astype(F32) + dot(set_attended.astype(BF16), wso[...])
    set_out[...] = states[:cells].astype(BF16)


def on_device(
    n, m, gene_tokens, latents, head_temp, w_key, w_value, w_out, w_set_qkv, w_set_out, set_ids
):
    cells, genes, width = gene_tokens.shape
    rows = latents.shape[0]
    portion = rows // n
    hbm = pl.BlockSpec(memory_space=pltpu.HBM)
    smem = pl.BlockSpec(memory_space=pltpu.SMEM)
    vmem = pl.BlockSpec(memory_space=pltpu.VMEM)
    wide = width + LANES
    return tuple(
        pl.pallas_call(
            functools.partial(kernel, n, m),
            out_shape=(
                jax.ShapeDtypeStruct((cells, portion, width), BF16),
                jax.ShapeDtypeStruct((cells, width), BF16),
            ),
            in_specs=[hbm, hbm, smem, hbm, hbm, hbm, hbm, hbm, smem],
            out_specs=(vmem, vmem),
            scratch_shapes=[
                pltpu.VMEM(gene_tokens.shape, BF16),
                pltpu.VMEM(latents.shape, BF16),
                pltpu.VMEM(w_key.shape, BF16),
                pltpu.VMEM(w_value.shape, BF16),
                pltpu.VMEM(w_out.shape, BF16),
                pltpu.VMEM(w_set_qkv.shape, BF16),
                pltpu.VMEM(w_set_out.shape, BF16),
                pltpu.VMEM((width // GROUP, GROUP, GROUP), BF16),
                pltpu.VMEM((cells, n, portion, wide), BF16),
                pltpu.VMEM((cells, n, portion, wide), BF16),
                pltpu.VMEM((cells * portion, wide), F32),
                pltpu.VMEM((ROWS, width // 2), F32),
                pltpu.VMEM((ROWS, width // 2), BF16),
                pltpu.VMEM((n, ROWS, width // 2), BF16),
                pltpu.VMEM((ROWS, wide), F32),
                pltpu.VMEM((m, ROWS, wide), F32),
                pltpu.SemaphoreType.DMA((6,)),
                pltpu.SemaphoreType.DMA((cells,)),
                pltpu.SemaphoreType.DMA((cells,)),
                pltpu.SemaphoreType.DMA((cells,)),
                pltpu.SemaphoreType.DMA((4,)),
            ],
            compiler_params=pltpu.CompilerParams(
                collective_id=0, has_side_effects=True, vmem_limit_bytes=50 * 1024 * 1024
            ),
            name="latent_cross_attention",
        )(gene_tokens, latents, head_temp, w_key, w_value, w_out, w_set_qkv, w_set_out, set_ids)
    )


def solution(mesh):
    n, m = mesh.shape["gene"], mesh.shape["cell"]
    in_specs = (P("cell", "gene", None), P(), P(), P(), P(), P(), P(), P(), P("cell"))
    out_specs = (P("cell", "gene", None), P("cell", None))
    return jax.shard_map(
        functools.partial(on_device, n, m),
        mesh=mesh,
        in_specs=in_specs,
        out_specs=out_specs,
        check_vma=False,
    )
```

```python
import functools
import math

import jax
import jax.numpy as jnp
from jax import lax
from jax.experimental import pallas as pl
from jax.experimental.pallas import tpu as pltpu
from jax.sharding import PartitionSpec as P

EPSILON = 1e-06
MESH = pl.DeviceIdType.MESH
F32, BF16 = jnp.float32, jnp.bfloat16
HEAD = 64
LANES = 128
GROUP = 256
VMEM_BYTES = 63 * 1024 * 1024
ROWS = 8


def iota(shape, dim):
    return lax.broadcasted_iota(jnp.int32, shape, dim)


def dot(a, b):
    return jnp.dot(a, b, preferred_element_type=F32)


def dot_nt(a, b):
    return lax.dot_general(a, b, (((1,), (1,)), ((), ())), preferred_element_type=F32)


def dot_split(a, b):
    high = a.astype(BF16)
    low = (a - high.astype(F32)).astype(BF16)
    return dot(high, b) + dot(low, b)


def kernel(
    n,
    m,
    tok_hbm,
    lat_hbm,
    temp_hbm,
    wk_hbm,
    wv_hbm,
    wo_hbm,
    wqkv_hbm,
    wso_hbm,
    ids_hbm,
    lat_out,
    set_out,
    tok,
    lat,
    wk,
    wv,
    wo,
    wqkv,
    wso,
    qb,
    send,
    recv,
    acc,
    psum,
    psend,
    precv,
    ssend,
    srecv,
    temp_ref,
    ids_ref,
    in_sem,
    tok_sem,
    send_sem,
    recv_sem,
    late_sem,
):
    cells, genes, width = tok.shape
    latents = lat.shape[0]
    portion = latents // n
    heads = width // HEAD
    groups = width // GROUP
    per_group = GROUP // HEAD
    half = width // 2
    gene = lax.axis_index("gene")
    cell = lax.axis_index("cell")

    barrier = pltpu.get_barrier_semaphore()
    for o in range(1, n):
        pl.semaphore_signal(
            barrier, inc=1, device_id=(lax.rem(gene + o, n), cell), device_id_type=MESH
        )
    for o in range(1, m):
        pl.semaphore_signal(
            barrier, inc=1, device_id=(gene, lax.rem(cell + o, m)), device_id_type=MESH
        )

    lat_in = pltpu.make_async_copy(lat_hbm, lat, in_sem.at[0])
    wk_in = pltpu.make_async_copy(wk_hbm, wk, in_sem.at[1])
    wv_in = pltpu.make_async_copy(wv_hbm, wv, in_sem.at[2])
    wo_in = pltpu.make_async_copy(wo_hbm, wo, in_sem.at[3])
    wqkv_in = pltpu.make_async_copy(wqkv_hbm, wqkv, in_sem.at[4])
    wso_in = pltpu.make_async_copy(wso_hbm, wso, in_sem.at[5])
    temp_in = pltpu.make_async_copy(temp_hbm, temp_ref, in_sem.at[6])
    ids_in = pltpu.make_async_copy(ids_hbm, ids_ref, in_sem.at[7])

    def tok_in(c):
        return pltpu.make_async_copy(tok_hbm.at[c], tok.at[c], tok_sem.at[c])

    lat_in.start()
    temp_in.start()
    ids_in.start()
    wk_in.start()
    tok_in(0).start()
    wv_in.start()
    for c in range(1, cells):
        tok_in(c).start()
    wo_in.start()
    wqkv_in.start()
    wso_in.start()

    same_head = (iota((GROUP, GROUP), 0) >> 6) == (iota((GROUP, GROUP), 1) >> 6)
    mean_head = jnp.where(same_head, 1.0 / HEAD, 0.0).astype(BF16)
    col_head = iota((latents, GROUP), 1) >> 6
    lane = iota((latents, LANES), 1)

    def head_scale(x):
        return lax.rsqrt(dot((x * x).astype(BF16), mean_head) + EPSILON)

    lat_in.wait()
    temp_in.wait()
    ids_in.wait()
    for i in range(groups):
        block = lat[:, i * GROUP : (i + 1) * GROUP].astype(F32)
        mean_square = dot_split(block * block, mean_head)
        temp = jnp.zeros((latents, GROUP), F32)
        for h in range(per_group):
            temp = jnp.where(
                col_head == h, temp_ref[i * per_group + h] / math.sqrt(HEAD), temp
            )
        query = block * lax.rsqrt(mean_square + EPSILON) * temp
        stacked = jnp.concatenate([query] * per_group, axis=0)
        qb[i] = jnp.where(same_head, stacked, 0.0).astype(BF16)

    wk_in.wait()
    wv_in.wait()
    pl.semaphore_wait(barrier, n - 1 + m - 1)

    def one_cell(c, carry):
        tok_in(c).wait()
        tokens = tok[c]
        totals = jnp.zeros((latents, LANES), F32)
        for i in range(groups):
            cols = slice(i * GROUP, (i + 1) * GROUP)
            key = dot(tokens, wk[:, cols])
            key = (key * head_scale(key)).astype(BF16)
            weights = jnp.exp(dot_nt(qb[i], key))
            value = dot(tokens, wv[:, cols]).astype(BF16)
            mixed = dot(weights.astype(BF16), value)
            total = jnp.sum(weights, axis=1, keepdims=True)
            numerator = mixed[:latents]
            for h in range(per_group):
                rows = slice(h * latents, (h + 1) * latents)
                numerator = jnp.where(col_head == h, mixed[rows], numerator)
                totals = jnp.where(lane == i * per_group + h, total[rows], totals)
            for j in range(n):
                send[c, j, :, cols] = numerator[j * portion : (j + 1) * portion].astype(BF16)
        for j in range(n):
            send[c, j, :, width:] = totals[j * portion : (j + 1) * portion].astype(BF16)
        for o in range(1, n):
            peer = lax.rem(gene + o, n)
            pltpu.make_async_remote_copy(
                src_ref=send.at[c, peer],
                dst_ref=recv.at[c, o],
                send_sem=send_sem.at[c],
                recv_sem=recv_sem.at[c],
                device_id=(peer, cell),
                device_id_type=MESH,
            ).start()
        return carry

    lax.fori_loop(0, cells, one_cell, 0)

    select = iota((cells * portion, latents), 0)
    select = lax.rem(select, portion) + gene * portion == iota((cells * portion, latents), 1)
    own_latents = dot(select.astype(F32).astype(BF16), lat[...])
    mean_latents = jnp.sum(lat[...].astype(F32), axis=0, keepdims=True) * (1.0 / latents)
    expand = iota((LANES, width), 0) == (iota((LANES, width), 1) >> 6)
    expand = expand.astype(F32).astype(BF16)
    one_hot = jnp.zeros((ROWS, LANES), F32)
    row8, lane8 = iota((ROWS, LANES), 0), iota((ROWS, LANES), 1)
    for c in range(cells):
        one_hot = jnp.where((row8 == c) & (lane8 == ids_ref[c]), 1.0, one_hot)

    for c in range(cells):
        arrived = pltpu.make_async_remote_copy(
            src_ref=send.at[c, pl.ds(0, n - 1)],
            dst_ref=recv.at[c, pl.ds(1, n - 1)],
            send_sem=send_sem.at[c],
            recv_sem=recv_sem.at[c],
            device_id=(gene, cell),
            device_id_type=MESH,
        )
        arrived.wait_recv()
        total = send[c, gene].astype(F32)
        for o in range(1, n):
            total = total + recv[c, o].astype(F32)
        acc[c * portion : (c + 1) * portion, :] = total
        arrived.wait_send()
    totals = acc[:, width:]
    is_head = iota(totals.shape, 1) < heads
    inverse = jnp.where(is_head, 1.0 / jnp.where(is_head, totals, 1.0), 0.0)
    attended = (acc[:, :width] * dot_split(inverse, expand)).astype(BF16)
    wide = attended.astype(F32)
    for c in range(cells):
        row = jnp.sum(wide[c * portion : (c + 1) * portion], axis=0, keepdims=True)
        psum[c : c + 1, :] = row[:, :half]
        psum[cells + c : cells + c + 1, :] = row[:, half:]
    psend[...] = psum[...].astype(BF16)
    for o in range(1, n):
        pltpu.make_async_remote_copy(
            src_ref=psend,
            dst_ref=precv.at[o],
            send_sem=late_sem.at[0],
            recv_sem=late_sem.at[1],
            device_id=(lax.rem(gene + o, n), cell),
            device_id_type=MESH,
        ).start()

    wo_in.wait()
    mixed_rows = own_latents + dot(attended, wo[...])
    for c in range(cells):
        lat_out[c] = mixed_rows[c * portion : (c + 1) * portion].astype(BF16)

    wqkv_in.wait()
    wso_in.wait()
    arrived = pltpu.make_async_remote_copy(
        src_ref=precv.at[pl.ds(1, n - 1)],
        dst_ref=precv.at[pl.ds(1, n - 1)],
        send_sem=late_sem.at[0],
        recv_sem=late_sem.at[1],
        device_id=(gene, cell),
        device_id_type=MESH,
    )
    arrived.wait_recv()
    summed = psend[...].astype(F32)
    for o in range(1, n):
        summed = summed + precv[o].astype(F32)
    arrived.wait_send()
    summed = jnp.concatenate([summed, pltpu.roll(summed, ROWS - cells, 0)], axis=1)
    pooled = mean_latents + dot_split(summed * (1.0 / latents), wo[...])
    scale = lax.rsqrt(jnp.mean(pooled * pooled, axis=1, keepdims=True) + EPSILON)
    own_input = (pooled * scale).astype(BF16)
    ssend[:, :width] = own_input.astype(F32)
    ssend[:, width:] = one_hot
    for o in range(1, m):
        pltpu.make_async_remote_copy(
            src_ref=ssend,
            dst_ref=srecv.at[o],
            send_sem=late_sem.at[2],
            recv_sem=late_sem.at[3],
            device_id=(gene, lax.rem(cell + o, m)),
            device_id_type=MESH,
        ).start()

    def head_rows(x):
        parts = []
        for i in range(groups):
            part = x[:, i * GROUP : (i + 1) * GROUP]
            parts.append(part * head_scale(part))
        return jnp.concatenate(parts, axis=1)

    stack = (heads * ROWS, width)
    own_head = (iota(stack, 0) >> 3) == (iota(stack, 1) >> 6)
    queries = head_rows(dot(own_input, wqkv[:, :width])) * (1.0 / math.sqrt(HEAD))
    queries = jnp.concatenate([queries] * heads, axis=0)
    queries = jnp.where(own_head, queries, 0.0).astype(BF16)
    query_sets = jnp.concatenate([one_hot] * heads, axis=0).astype(BF16)

    arrived = pltpu.make_async_remote_copy(
        src_ref=srecv.at[pl.ds(1, m - 1)],
        dst_ref=srecv.at[pl.ds(1, m - 1)],
        send_sem=late_sem.at[2],
        recv_sem=late_sem.at[3],
        device_id=(gene, cell),
        device_id_type=MESH,
    )
    arrived.wait_recv()
    every = jnp.concatenate([ssend[...]] + [srecv[o] for o in range(1, m)], axis=0).astype(BF16)
    arrived.wait_send()
    every_input, key_sets = every[:, :width], every[:, width:]
    keys_values = dot(every_input, wqkv[:, width:])
    keys = head_rows(keys_values[:, :width]).astype(BF16)
    values = keys_values[:, width:].astype(BF16)
    matching = dot_nt(query_sets, key_sets) > 0.5
    weights = jnp.where(matching, jnp.exp(dot_nt(queries, keys)), 0.0)
    total = jnp.sum(weights, axis=1, keepdims=True)
    total = jnp.where(total > 0.0, total, 1.0)
    mixed = jnp.where(own_head, dot(weights.astype(BF16), values) / total, 0.0)
    set_attended = mixed[:ROWS]
    for h in range(1, heads):
        set_attended = set_attended + mixed[h * ROWS : (h + 1) * ROWS]
    states = own_input.astype(F32) + dot(set_attended.astype(BF16), wso[...])
    set_out[...] = states[:cells].astype(BF16)


def on_device(
    n, m, gene_tokens, latents, head_temp, w_key, w_value, w_out, w_set_qkv, w_set_out, set_ids
):
    cells, genes, width = gene_tokens.shape
    rows = latents.shape[0]
    portion = rows // n
    hbm = pl.BlockSpec(memory_space=pltpu.HBM)
    vmem = pl.BlockSpec(memory_space=pltpu.VMEM)
    wide = width + LANES
    return tuple(
        pl.pallas_call(
            functools.partial(kernel, n, m),
            out_shape=(
                jax.ShapeDtypeStruct((cells, portion, width), BF16),
                jax.ShapeDtypeStruct((cells, width), BF16),
            ),
            in_specs=[hbm] * 9,
            out_specs=(vmem, vmem),
            scratch_shapes=[
                pltpu.VMEM(gene_tokens.shape, BF16),
                pltpu.VMEM(latents.shape, BF16),
                pltpu.VMEM(w_key.shape, BF16),
                pltpu.VMEM(w_value.shape, BF16),
                pltpu.VMEM(w_out.shape, BF16),
                pltpu.VMEM(w_set_qkv.shape, BF16),
                pltpu.VMEM(w_set_out.shape, BF16),
                pltpu.VMEM((width // GROUP, GROUP, GROUP), BF16),
                pltpu.VMEM((cells, n, portion, wide), BF16),
                pltpu.VMEM((cells, n, portion, wide), BF16),
                pltpu.VMEM((cells * portion, wide), F32),
                pltpu.VMEM((ROWS, width // 2), F32),
                pltpu.VMEM((ROWS, width // 2), BF16),
                pltpu.VMEM((n, ROWS, width // 2), BF16),
                pltpu.VMEM((ROWS, wide), F32),
                pltpu.VMEM((m, ROWS, wide), F32),
                pltpu.SMEM(head_temp.shape, F32),
                pltpu.SMEM(set_ids.shape, jnp.int32),
                pltpu.SemaphoreType.DMA((8,)),
                pltpu.SemaphoreType.DMA((cells,)),
                pltpu.SemaphoreType.DMA((cells,)),
                pltpu.SemaphoreType.DMA((cells,)),
                pltpu.SemaphoreType.DMA((4,)),
            ],
            compiler_params=pltpu.CompilerParams(
                collective_id=0, has_side_effects=True, vmem_limit_bytes=VMEM_BYTES
            ),
            name="latent_cross_attention",
        )(gene_tokens, latents, head_temp, w_key, w_value, w_out, w_set_qkv, w_set_out, set_ids)
    )


def solution(mesh):
    n, m = mesh.shape["gene"], mesh.shape["cell"]
    in_specs = (P("cell", "gene", None), P(), P(), P(), P(), P(), P(), P(), P("cell"))
    out_specs = (P("cell", "gene", None), P("cell", None))
    return jax.shard_map(
        functools.partial(on_device, n, m),
        mesh=mesh,
        in_specs=in_specs,
        out_specs=out_specs,
        check_vma=False,
    )
```

```python
import functools
import math

import jax
import jax.numpy as jnp
from jax import lax
from jax.experimental import pallas as pl
from jax.experimental.pallas import tpu as pltpu
from jax.sharding import PartitionSpec as P

EPSILON = 1e-06
MESH = pl.DeviceIdType.MESH
F32, BF16 = jnp.float32, jnp.bfloat16
HEAD = 64
LANES = 128
GROUP = 256
VMEM_BYTES = 63 * 1024 * 1024
ROWS = 8


def iota(shape, dim):
    return lax.broadcasted_iota(jnp.int32, shape, dim)


def dot(a, b):
    return jnp.dot(a, b, preferred_element_type=F32)


def dot_nt(a, b):
    return lax.dot_general(a, b, (((1,), (1,)), ((), ())), preferred_element_type=F32)


def dot_split(a, b):
    high = a.astype(BF16)
    low = (a - high.astype(F32)).astype(BF16)
    both = dot(jnp.concatenate([high, low], axis=0), b)
    return both[: a.shape[0]] + both[a.shape[0] :]


def kernel(
    n,
    m,
    tok_hbm,
    lat_hbm,
    temp_hbm,
    wk_hbm,
    wv_hbm,
    wo_hbm,
    wqkv_hbm,
    wso_hbm,
    ids_hbm,
    lat_out,
    set_out,
    tok,
    lat,
    wk,
    wv,
    wo,
    wqkv,
    wso,
    qb,
    send,
    recv,
    acc,
    psum,
    psend,
    precv,
    ssend,
    srecv,
    tsend,
    trecv,
    hsend,
    hrecv,
    inv,
    temp_ref,
    ids_ref,
    in_sem,
    tok_sem,
    send_sem,
    recv_sem,
    late_sem,
):
    cells, genes, width = tok.shape
    latents = lat.shape[0]
    portion = latents // n
    heads = width // HEAD
    groups = width // GROUP
    per_group = GROUP // HEAD
    half = width // 2
    gene = lax.axis_index("gene")
    cell = lax.axis_index("cell")

    barrier = pltpu.get_barrier_semaphore()
    for o in range(1, n):
        pl.semaphore_signal(
            barrier, inc=1, device_id=(lax.rem(gene + o, n), cell), device_id_type=MESH
        )
    for o in range(1, m):
        pl.semaphore_signal(
            barrier, inc=1, device_id=(gene, lax.rem(cell + o, m)), device_id_type=MESH
        )

    lat_in = pltpu.make_async_copy(lat_hbm, lat, in_sem.at[0])
    wk_in = pltpu.make_async_copy(wk_hbm, wk, in_sem.at[1])
    wv_in = pltpu.make_async_copy(wv_hbm, wv, in_sem.at[2])
    wo_in = pltpu.make_async_copy(wo_hbm, wo, in_sem.at[3])
    wqkv_in = pltpu.make_async_copy(wqkv_hbm, wqkv, in_sem.at[4])
    wso_in = pltpu.make_async_copy(wso_hbm, wso, in_sem.at[5])
    temp_in = pltpu.make_async_copy(temp_hbm, temp_ref, in_sem.at[6])
    ids_in = pltpu.make_async_copy(ids_hbm, ids_ref, in_sem.at[7])

    def tok_in(c):
        return pltpu.make_async_copy(tok_hbm.at[c], tok.at[c], tok_sem.at[c])

    lat_in.start()
    temp_in.start()
    ids_in.start()
    wk_in.start()
    tok_in(0).start()
    wv_in.start()
    for c in range(1, cells):
        tok_in(c).start()
    wo_in.start()
    wqkv_in.start()
    wso_in.start()

    same_head = (iota((GROUP, GROUP), 0) >> 6) == (iota((GROUP, GROUP), 1) >> 6)
    mean_head = jnp.where(same_head, 1.0 / HEAD, 0.0).astype(BF16)
    col_head = iota((latents, GROUP), 1) >> 6
    lane = iota((latents, LANES), 1)

    def side_by_side(x):
        return jnp.concatenate([x, pltpu.roll(x, ROWS - cells, 0)], axis=1)

    def head_scale(x):
        return lax.rsqrt(dot((x * x).astype(BF16), mean_head) + EPSILON)

    lat_in.wait()
    temp_in.wait()
    ids_in.wait()
    for i in range(groups):
        block = lat[:, i * GROUP : (i + 1) * GROUP].astype(F32)
        mean_square = dot_split(block * block, mean_head)
        temp = jnp.zeros((latents, GROUP), F32)
        for h in range(per_group):
            temp = jnp.where(
                col_head == h, temp_ref[i * per_group + h] / math.sqrt(HEAD), temp
            )
        query = block * lax.rsqrt(mean_square + EPSILON) * temp
        stacked = jnp.concatenate([query] * per_group, axis=0)
        qb[i] = jnp.where(same_head, stacked, 0.0).astype(BF16)

    wk_in.wait()
    wv_in.wait()
    one_hot = jnp.zeros((ROWS, LANES), F32)
    row8, lane8 = iota((ROWS, LANES), 0), iota((ROWS, LANES), 1)
    for c in range(cells):
        one_hot = jnp.where((row8 == c) & (lane8 == ids_ref[c]), 1.0, one_hot)
    hsend[...] = one_hot
    pl.semaphore_wait(barrier, n - 1 + m - 1)
    for o in range(1, m):
        pltpu.make_async_remote_copy(
            src_ref=hsend,
            dst_ref=hrecv.at[o],
            send_sem=late_sem.at[4],
            recv_sem=late_sem.at[5],
            device_id=(gene, lax.rem(cell + o, m)),
            device_id_type=MESH,
        ).start()

    spans = [slice(i * GROUP, (i + 1) * GROUP) for i in range(groups)]

    def one_cell(c, totals):
        tok_in(c).wait()
        tokens = tok[c]
        raw = dot(tokens, wk[...])
        squares = (raw * raw).astype(BF16)
        values = dot(tokens, wv[...]).astype(BF16)
        scales = [lax.rsqrt(dot(squares[:, s], mean_head) + EPSILON) for s in spans]
        keys = [(raw[:, s] * scale).astype(BF16) for s, scale in zip(spans, scales)]
        weights = [jnp.exp(dot_nt(qb[i], keys[i])) for i in range(groups)]
        mixes = [dot(weights[i].astype(BF16), values[:, spans[i]]) for i in range(groups)]
        for i in range(groups):
            mixed = mixes[i]
            total = jnp.sum(weights[i], axis=1, keepdims=True)
            numerator = mixed[:latents]
            for h in range(per_group):
                rows = slice(h * latents, (h + 1) * latents)
                numerator = jnp.where(col_head == h, mixed[rows], numerator)
                place = c * heads + i * per_group + h
                totals = jnp.where(lane == place, total[rows], totals)
            for j in range(n):
                send[c, j, :, spans[i]] = numerator[j * portion : (j + 1) * portion].astype(BF16)
        for o in range(1, n):
            peer = lax.rem(gene + o, n)
            pltpu.make_async_remote_copy(
                src_ref=send.at[c, peer],
                dst_ref=recv.at[c, o],
                send_sem=send_sem.at[c],
                recv_sem=recv_sem.at[c],
                device_id=(peer, cell),
                device_id_type=MESH,
            ).start()
        return totals

    totals = lax.fori_loop(0, cells, one_cell, jnp.zeros((latents, LANES), F32))
    for j in range(n):
        tsend[j] = totals[j * portion : (j + 1) * portion].astype(BF16)
    for o in range(1, n):
        peer = lax.rem(gene + o, n)
        pltpu.make_async_remote_copy(
            src_ref=tsend.at[peer],
            dst_ref=trecv.at[o],
            send_sem=late_sem.at[6],
            recv_sem=late_sem.at[7],
            device_id=(peer, cell),
            device_id_type=MESH,
        ).start()

    select = iota((cells * portion, latents), 0)
    select = lax.rem(select, portion) + gene * portion == iota((cells * portion, latents), 1)
    own_latents = dot(select.astype(F32).astype(BF16), lat[...])
    mean_latents = jnp.sum(lat[...].astype(F32), axis=0, keepdims=True) * (1.0 / latents)
    expand = lax.rem(iota((LANES, width), 0), heads) == (iota((LANES, width), 1) >> 6)
    expand = expand.astype(F32).astype(BF16)

    for c in range(cells):
        arrived = pltpu.make_async_remote_copy(
            src_ref=send.at[c, pl.ds(0, n - 1)],
            dst_ref=recv.at[c, pl.ds(1, n - 1)],
            send_sem=send_sem.at[c],
            recv_sem=recv_sem.at[c],
            device_id=(gene, cell),
            device_id_type=MESH,
        )
        arrived.wait_recv()
        total = send[c, gene].astype(F32)
        for o in range(1, n):
            total = total + recv[c, o].astype(F32)
        acc[c * portion : (c + 1) * portion, :] = total
        arrived.wait_send()
    arrived = pltpu.make_async_remote_copy(
        src_ref=trecv.at[pl.ds(1, n - 1)],
        dst_ref=trecv.at[pl.ds(1, n - 1)],
        send_sem=late_sem.at[6],
        recv_sem=late_sem.at[7],
        device_id=(gene, cell),
        device_id_type=MESH,
    )
    arrived.wait_recv()
    totals = tsend[gene].astype(F32)
    for o in range(1, n):
        totals = totals + trecv[o].astype(F32)
    arrived.wait_send()
    place = iota((portion, LANES), 1)
    inverse = 1.0 / jnp.where(place < cells * heads, totals, 1.0)
    for c in range(cells):
        own = (place >= c * heads) & (place < (c + 1) * heads)
        inv[c * portion : (c + 1) * portion, :] = jnp.where(own, inverse, 0.0)
    attended = (acc[...] * dot_split(inv[...], expand)).astype(BF16)
    wide = attended.astype(F32)
    for c in range(cells):
        row = jnp.sum(wide[c * portion : (c + 1) * portion], axis=0, keepdims=True)
        psum[c : c + 1, :] = row[:, :half]
        psum[cells + c : cells + c + 1, :] = row[:, half:]
    psend[...] = psum[...].astype(BF16)
    for o in range(1, n):
        pltpu.make_async_remote_copy(
            src_ref=psend,
            dst_ref=precv.at[o],
            send_sem=late_sem.at[0],
            recv_sem=late_sem.at[1],
            device_id=(lax.rem(gene + o, n), cell),
            device_id_type=MESH,
        ).start()

    wo_in.wait()
    mixed_rows = own_latents + dot(attended, wo[...])
    for c in range(cells):
        lat_out[c] = mixed_rows[c * portion : (c + 1) * portion].astype(BF16)

    wqkv_in.wait()
    wso_in.wait()
    arrived = pltpu.make_async_remote_copy(
        src_ref=precv.at[pl.ds(1, n - 1)],
        dst_ref=precv.at[pl.ds(1, n - 1)],
        send_sem=late_sem.at[0],
        recv_sem=late_sem.at[1],
        device_id=(gene, cell),
        device_id_type=MESH,
    )
    arrived.wait_recv()
    summed = psend[...].astype(F32)
    for o in range(1, n):
        summed = summed + precv[o].astype(F32)
    arrived.wait_send()
    pooled = mean_latents + dot_split(side_by_side(summed) * (1.0 / latents), wo[...])
    scale = lax.rsqrt(jnp.mean(pooled * pooled, axis=1, keepdims=True) + EPSILON)
    own_input = (pooled * scale).astype(BF16)
    own_wide = own_input.astype(F32)
    second = pltpu.roll(own_wide[:, half:], cells, 0)
    ssend[...] = jnp.where(iota((ROWS, half), 0) < cells, own_wide[:, :half], second).astype(BF16)
    for o in range(1, m):
        pltpu.make_async_remote_copy(
            src_ref=ssend,
            dst_ref=srecv.at[o],
            send_sem=late_sem.at[2],
            recv_sem=late_sem.at[3],
            device_id=(gene, lax.rem(cell + o, m)),
            device_id_type=MESH,
        ).start()

    def head_rows(x):
        parts = []
        for i in range(groups):
            part = x[:, i * GROUP : (i + 1) * GROUP]
            parts.append(part * head_scale(part))
        return jnp.concatenate(parts, axis=1)

    stack = (heads * ROWS, width)
    own_head = (iota(stack, 0) >> 3) == (iota(stack, 1) >> 6)
    queries = head_rows(dot(own_input, wqkv[:, :width])) * (1.0 / math.sqrt(HEAD))
    queries = jnp.concatenate([queries] * heads, axis=0)
    queries = jnp.where(own_head, queries, 0.0).astype(BF16)
    query_sets = jnp.concatenate([one_hot] * heads, axis=0).astype(BF16)

    arrived = pltpu.make_async_remote_copy(
        src_ref=srecv.at[pl.ds(1, m - 1)],
        dst_ref=srecv.at[pl.ds(1, m - 1)],
        send_sem=late_sem.at[2],
        recv_sem=late_sem.at[3],
        device_id=(gene, cell),
        device_id_type=MESH,
    )
    arrived.wait_recv()
    parts = [own_wide] + [side_by_side(srecv[o].astype(F32)) for o in range(1, m)]
    every_input = jnp.concatenate(parts, axis=0).astype(BF16)
    arrived.wait_send()
    arrived = pltpu.make_async_remote_copy(
        src_ref=hrecv.at[pl.ds(1, m - 1)],
        dst_ref=hrecv.at[pl.ds(1, m - 1)],
        send_sem=late_sem.at[4],
        recv_sem=late_sem.at[5],
        device_id=(gene, cell),
        device_id_type=MESH,
    )
    arrived.wait_recv()
    key_sets = jnp.concatenate([one_hot] + [hrecv[o] for o in range(1, m)], axis=0).astype(BF16)
    arrived.wait_send()
    keys_values = dot(every_input, wqkv[:, width:])
    keys = head_rows(keys_values[:, :width]).astype(BF16)
    values = keys_values[:, width:].astype(BF16)
    matching = dot_nt(query_sets, key_sets) > 0.5
    weights = jnp.where(matching, jnp.exp(dot_nt(queries, keys)), 0.0)
    total = jnp.sum(weights, axis=1, keepdims=True)
    total = jnp.where(total > 0.0, total, 1.0)
    mixed = jnp.where(own_head, dot(weights.astype(BF16), values) / total, 0.0)
    set_attended = mixed[:ROWS]
    for h in range(1, heads):
        set_attended = set_attended + mixed[h * ROWS : (h + 1) * ROWS]
    states = own_input.astype(F32) + dot(set_attended.astype(BF16), wso[...])
    set_out[...] = states[:cells].astype(BF16)


def on_device(
    n, m, gene_tokens, latents, head_temp, w_key, w_value, w_out, w_set_qkv, w_set_out, set_ids
):
    cells, genes, width = gene_tokens.shape
    rows = latents.shape[0]
    portion = rows // n
    hbm = pl.BlockSpec(memory_space=pltpu.HBM)
    vmem = pl.BlockSpec(memory_space=pltpu.VMEM)
    return tuple(
        pl.pallas_call(
            functools.partial(kernel, n, m),
            out_shape=(
                jax.ShapeDtypeStruct((cells, portion, width), BF16),
                jax.ShapeDtypeStruct((cells, width), BF16),
            ),
            in_specs=[hbm] * 9,
            out_specs=(vmem, vmem),
            scratch_shapes=[
                pltpu.VMEM(gene_tokens.shape, BF16),
                pltpu.VMEM(latents.shape, BF16),
                pltpu.VMEM(w_key.shape, BF16),
                pltpu.VMEM(w_value.shape, BF16),
                pltpu.VMEM(w_out.shape, BF16),
                pltpu.VMEM(w_set_qkv.shape, BF16),
                pltpu.VMEM(w_set_out.shape, BF16),
                pltpu.VMEM((width // GROUP, GROUP, GROUP), BF16),
                pltpu.VMEM((cells, n, portion, width), BF16),
                pltpu.VMEM((cells, n, portion, width), BF16),
                pltpu.VMEM((cells * portion, width), F32),
                pltpu.VMEM((ROWS, width // 2), F32),
                pltpu.VMEM((ROWS, width // 2), BF16),
                pltpu.VMEM((n, ROWS, width // 2), BF16),
                pltpu.VMEM((ROWS, width // 2), BF16),
                pltpu.VMEM((m, ROWS, width // 2), BF16),
                pltpu.VMEM((n, portion, LANES), BF16),
                pltpu.VMEM((n, portion, LANES), BF16),
                pltpu.VMEM((ROWS, LANES), F32),
                pltpu.VMEM((m, ROWS, LANES), F32),
                pltpu.VMEM((cells * portion, LANES), F32),
                pltpu.SMEM(head_temp.shape, F32),
                pltpu.SMEM(set_ids.shape, jnp.int32),
                pltpu.SemaphoreType.DMA((8,)),
                pltpu.SemaphoreType.DMA((cells,)),
                pltpu.SemaphoreType.DMA((cells,)),
                pltpu.SemaphoreType.DMA((cells,)),
                pltpu.SemaphoreType.DMA((8,)),
            ],
            compiler_params=pltpu.CompilerParams(
                collective_id=0, has_side_effects=True, vmem_limit_bytes=VMEM_BYTES
            ),
            name="latent_cross_attention",
        )(gene_tokens, latents, head_temp, w_key, w_value, w_out, w_set_qkv, w_set_out, set_ids)
    )


def solution(mesh):
    n, m = mesh.shape["gene"], mesh.shape["cell"]
    in_specs = (P("cell", "gene", None), P(), P(), P(), P(), P(), P(), P(), P("cell"))
    out_specs = (P("cell", "gene", None), P("cell", None))
    return jax.shard_map(
        functools.partial(on_device, n, m),
        mesh=mesh,
        in_specs=in_specs,
        out_specs=out_specs,
        check_vma=False,
    )
```

```python
import functools
import math

import jax
import jax.numpy as jnp
from jax import lax
from jax.experimental import pallas as pl
from jax.experimental.pallas import tpu as pltpu
from jax.sharding import PartitionSpec as P

EPSILON = 1e-06
MESH = pl.DeviceIdType.MESH
F32, BF16 = jnp.float32, jnp.bfloat16
HEAD = 64
LANES = 128
GROUP = 256
VMEM_BYTES = 58 * 1024 * 1024
ROWS = 8


def iota(shape, dim):
    return lax.broadcasted_iota(jnp.int32, shape, dim)


def dot(a, b):
    return jnp.dot(a, b, preferred_element_type=F32)


def dot_nt(a, b):
    return lax.dot_general(a, b, (((1,), (1,)), ((), ())), preferred_element_type=F32)


def dot_split(a, b):
    high = a.astype(BF16)
    low = (a - high.astype(F32)).astype(BF16)
    both = dot(jnp.concatenate([high, low], axis=0), b)
    return both[: a.shape[0]] + both[a.shape[0] :]


def kernel(
    n,
    m,
    tok_hbm,
    lat_hbm,
    temp_hbm,
    wk_hbm,
    wv_hbm,
    wo_hbm,
    wqkv_hbm,
    wso_hbm,
    ids_hbm,
    lat_out,
    set_out,
    tok,
    lat,
    wk,
    wv,
    wo,
    wqkv,
    wso,
    qb,
    send,
    recv,
    acc,
    psum,
    psend,
    precv,
    ssend,
    srecv,
    tsend,
    trecv,
    hsend,
    hrecv,
    inv,
    temp_ref,
    ids_ref,
    in_sem,
    tok_sem,
    send_sem,
    recv_sem,
    late_sem,
):
    cells, genes, width = tok.shape
    latents = lat.shape[0]
    portion = latents // n
    heads = width // HEAD
    groups = width // GROUP
    per_group = GROUP // HEAD
    half = width // 2
    gene = lax.axis_index("gene")
    cell = lax.axis_index("cell")

    barrier = pltpu.get_barrier_semaphore()
    for o in range(1, n):
        pl.semaphore_signal(
            barrier, inc=1, device_id=(lax.rem(gene + o, n), cell), device_id_type=MESH
        )
    for o in range(1, m):
        pl.semaphore_signal(
            barrier, inc=1, device_id=(gene, lax.rem(cell + o, m)), device_id_type=MESH
        )

    lat_in = pltpu.make_async_copy(lat_hbm, lat, in_sem.at[0])
    wk_in = pltpu.make_async_copy(wk_hbm, wk, in_sem.at[1])
    wv_in = pltpu.make_async_copy(wv_hbm, wv, in_sem.at[2])
    wo_in = pltpu.make_async_copy(wo_hbm, wo, in_sem.at[3])
    wqkv_in = pltpu.make_async_copy(wqkv_hbm, wqkv, in_sem.at[4])
    wso_in = pltpu.make_async_copy(wso_hbm, wso, in_sem.at[5])
    temp_in = pltpu.make_async_copy(temp_hbm, temp_ref, in_sem.at[6])
    ids_in = pltpu.make_async_copy(ids_hbm, ids_ref, in_sem.at[7])

    def tok_in(c):
        return pltpu.make_async_copy(tok_hbm.at[c], tok.at[c], tok_sem.at[c])

    lat_in.start()
    temp_in.start()
    ids_in.start()
    wk_in.start()
    tok_in(0).start()
    wv_in.start()
    for c in range(1, cells):
        tok_in(c).start()
    wo_in.start()
    wqkv_in.start()
    wso_in.start()

    same_head = (iota((GROUP, GROUP), 0) >> 6) == (iota((GROUP, GROUP), 1) >> 6)
    mean_head = jnp.where(same_head, 1.0 / HEAD, 0.0).astype(BF16)
    col_head = iota((latents, GROUP), 1) >> 6
    lane = iota((latents, LANES), 1)

    def side_by_side(x):
        return jnp.concatenate([x, pltpu.roll(x, ROWS - cells, 0)], axis=1)

    def head_scale(x):
        return lax.rsqrt(dot((x * x).astype(BF16), mean_head) + EPSILON)

    lat_in.wait()
    temp_in.wait()
    ids_in.wait()
    for i in range(groups):
        block = lat[:, i * GROUP : (i + 1) * GROUP].astype(F32)
        mean_square = dot_split(block * block, mean_head)
        temp = jnp.zeros((latents, GROUP), F32)
        for h in range(per_group):
            temp = jnp.where(
                col_head == h, temp_ref[i * per_group + h] / math.sqrt(HEAD), temp
            )
        query = block * lax.rsqrt(mean_square + EPSILON) * temp
        stacked = jnp.concatenate([query] * per_group, axis=0)
        qb[i] = jnp.where(same_head, stacked, 0.0).astype(BF16)

    wk_in.wait()
    wv_in.wait()
    one_hot = jnp.zeros((ROWS, LANES), F32)
    row8, lane8 = iota((ROWS, LANES), 0), iota((ROWS, LANES), 1)
    for c in range(cells):
        one_hot = jnp.where((row8 == c) & (lane8 == ids_ref[c]), 1.0, one_hot)
    hsend[...] = one_hot
    pl.semaphore_wait(barrier, n - 1 + m - 1)
    for o in range(1, m):
        pltpu.make_async_remote_copy(
            src_ref=hsend,
            dst_ref=hrecv.at[o],
            send_sem=late_sem.at[4],
            recv_sem=late_sem.at[5],
            device_id=(gene, lax.rem(cell + o, m)),
            device_id_type=MESH,
        ).start()

    spans = [slice(i * GROUP, (i + 1) * GROUP) for i in range(groups)]

    def one_cell(c, totals):
        tok_in(c).wait()
        tokens = tok[c]
        raw = dot(tokens, wk[...])
        squares = (raw * raw).astype(BF16)
        values = dot(tokens, wv[...]).astype(BF16)
        scales = [lax.rsqrt(dot(squares[:, s], mean_head) + EPSILON) for s in spans]
        keys = [(raw[:, s] * scale).astype(BF16) for s, scale in zip(spans, scales)]
        weights = [jnp.exp(dot_nt(qb[i], keys[i])) for i in range(groups)]
        mixes = [dot(weights[i].astype(BF16), values[:, spans[i]]) for i in range(groups)]
        for i in range(groups):
            mixed = mixes[i]
            total = jnp.sum(weights[i], axis=1, keepdims=True)
            numerator = mixed[:latents]
            for h in range(per_group):
                rows = slice(h * latents, (h + 1) * latents)
                numerator = jnp.where(col_head == h, mixed[rows], numerator)
                place = c * heads + i * per_group + h
                totals = jnp.where(lane == place, total[rows], totals)
            for j in range(n):
                send[c, j, :, spans[i]] = numerator[j * portion : (j + 1) * portion].astype(BF16)
        for o in range(1, n):
            peer = lax.rem(gene + o, n)
            pltpu.make_async_remote_copy(
                src_ref=send.at[c, peer],
                dst_ref=recv.at[c, o],
                send_sem=send_sem.at[c],
                recv_sem=recv_sem.at[c],
                device_id=(peer, cell),
                device_id_type=MESH,
            ).start()
        return totals

    totals = lax.fori_loop(0, cells, one_cell, jnp.zeros((latents, LANES), F32))
    for j in range(n):
        tsend[j] = totals[j * portion : (j + 1) * portion].astype(BF16)
    for o in range(1, n):
        peer = lax.rem(gene + o, n)
        pltpu.make_async_remote_copy(
            src_ref=tsend.at[peer],
            dst_ref=trecv.at[o],
            send_sem=late_sem.at[6],
            recv_sem=late_sem.at[7],
            device_id=(peer, cell),
            device_id_type=MESH,
        ).start()

    select = iota((cells * portion, latents), 0)
    select = lax.rem(select, portion) + gene * portion == iota((cells * portion, latents), 1)
    own_latents = dot(select.astype(F32).astype(BF16), lat[...])
    mean_latents = jnp.sum(lat[...].astype(F32), axis=0, keepdims=True) * (1.0 / latents)
    expand = lax.rem(iota((LANES, width), 0), heads) == (iota((LANES, width), 1) >> 6)
    expand = expand.astype(F32).astype(BF16)

    for c in range(cells):
        arrived = pltpu.make_async_remote_copy(
            src_ref=send.at[c, pl.ds(0, n - 1)],
            dst_ref=recv.at[c, pl.ds(1, n - 1)],
            send_sem=send_sem.at[c],
            recv_sem=recv_sem.at[c],
            device_id=(gene, cell),
            device_id_type=MESH,
        )
        arrived.wait_recv()
        total = send[c, gene].astype(F32)
        for o in range(1, n):
            total = total + recv[c, o].astype(F32)
        acc[c * portion : (c + 1) * portion, :] = total
        arrived.wait_send()
    arrived = pltpu.make_async_remote_copy(
        src_ref=trecv.at[pl.ds(1, n - 1)],
        dst_ref=trecv.at[pl.ds(1, n - 1)],
        send_sem=late_sem.at[6],
        recv_sem=late_sem.at[7],
        device_id=(gene, cell),
        device_id_type=MESH,
    )
    arrived.wait_recv()
    totals = tsend[gene].astype(F32)
    for o in range(1, n):
        totals = totals + trecv[o].astype(F32)
    arrived.wait_send()
    place = iota((portion, LANES), 1)
    inverse = 1.0 / jnp.where(place < cells * heads, totals, 1.0)
    for c in range(cells):
        own = (place >= c * heads) & (place < (c + 1) * heads)
        inv[c * portion : (c + 1) * portion, :] = jnp.where(own, inverse, 0.0)
    attended = (acc[...] * dot_split(inv[...], expand)).astype(BF16)
    wide = attended.astype(F32)
    for c in range(cells):
        row = jnp.sum(wide[c * portion : (c + 1) * portion], axis=0, keepdims=True)
        psum[c : c + 1, :] = row[:, :half]
        psum[cells + c : cells + c + 1, :] = row[:, half:]
    psend[...] = psum[...].astype(BF16)
    for o in range(1, n):
        pltpu.make_async_remote_copy(
            src_ref=psend,
            dst_ref=precv.at[o],
            send_sem=late_sem.at[0],
            recv_sem=late_sem.at[1],
            device_id=(lax.rem(gene + o, n), cell),
            device_id_type=MESH,
        ).start()

    wo_in.wait()
    mixed_rows = own_latents + dot(attended, wo[...])
    for c in range(cells):
        lat_out[c] = mixed_rows[c * portion : (c + 1) * portion].astype(BF16)

    wqkv_in.wait()
    wso_in.wait()
    arrived = pltpu.make_async_remote_copy(
        src_ref=precv.at[pl.ds(1, n - 1)],
        dst_ref=precv.at[pl.ds(1, n - 1)],
        send_sem=late_sem.at[0],
        recv_sem=late_sem.at[1],
        device_id=(gene, cell),
        device_id_type=MESH,
    )
    arrived.wait_recv()
    summed = psend[...].astype(F32)
    for o in range(1, n):
        summed = summed + precv[o].astype(F32)
    arrived.wait_send()
    pooled = mean_latents + dot_split(side_by_side(summed) * (1.0 / latents), wo[...])
    scale = lax.rsqrt(jnp.mean(pooled * pooled, axis=1, keepdims=True) + EPSILON)
    own_input = (pooled * scale).astype(BF16)
    own_wide = own_input.astype(F32)
    second = pltpu.roll(own_wide[:, half:], cells, 0)
    ssend[...] = jnp.where(iota((ROWS, half), 0) < cells, own_wide[:, :half], second).astype(BF16)
    for o in range(1, m):
        pltpu.make_async_remote_copy(
            src_ref=ssend,
            dst_ref=srecv.at[o],
            send_sem=late_sem.at[2],
            recv_sem=late_sem.at[3],
            device_id=(gene, lax.rem(cell + o, m)),
            device_id_type=MESH,
        ).start()

    def head_rows(x):
        parts = []
        for i in range(groups):
            part = x[:, i * GROUP : (i + 1) * GROUP]
            parts.append(part * head_scale(part))
        return jnp.concatenate(parts, axis=1)

    stack = (heads * ROWS, width)
    own_head = (iota(stack, 0) >> 3) == (iota(stack, 1) >> 6)
    queries = head_rows(dot(own_input, wqkv[:, :width])) * (1.0 / math.sqrt(HEAD))
    queries = jnp.concatenate([queries] * heads, axis=0)
    queries = jnp.where(own_head, queries, 0.0).astype(BF16)
    query_sets = jnp.concatenate([one_hot] * heads, axis=0).astype(BF16)

    arrived = pltpu.make_async_remote_copy(
        src_ref=srecv.at[pl.ds(1, m - 1)],
        dst_ref=srecv.at[pl.ds(1, m - 1)],
        send_sem=late_sem.at[2],
        recv_sem=late_sem.at[3],
        device_id=(gene, cell),
        device_id_type=MESH,
    )
    arrived.wait_recv()
    parts = [own_wide] + [side_by_side(srecv[o].astype(F32)) for o in range(1, m)]
    every_input = jnp.concatenate(parts, axis=0).astype(BF16)
    arrived.wait_send()
    arrived = pltpu.make_async_remote_copy(
        src_ref=hrecv.at[pl.ds(1, m - 1)],
        dst_ref=hrecv.at[pl.ds(1, m - 1)],
        send_sem=late_sem.at[4],
        recv_sem=late_sem.at[5],
        device_id=(gene, cell),
        device_id_type=MESH,
    )
    arrived.wait_recv()
    key_sets = jnp.concatenate([one_hot] + [hrecv[o] for o in range(1, m)], axis=0).astype(BF16)
    arrived.wait_send()
    keys_values = dot(every_input, wqkv[:, width:])
    keys = head_rows(keys_values[:, :width]).astype(BF16)
    values = keys_values[:, width:].astype(BF16)
    matching = dot_nt(query_sets, key_sets) > 0.5
    weights = jnp.where(matching, jnp.exp(dot_nt(queries, keys)), 0.0)
    total = jnp.sum(weights, axis=1, keepdims=True)
    total = jnp.where(total > 0.0, total, 1.0)
    mixed = jnp.where(own_head, dot(weights.astype(BF16), values) / total, 0.0)
    set_attended = mixed[:ROWS]
    for h in range(1, heads):
        set_attended = set_attended + mixed[h * ROWS : (h + 1) * ROWS]
    states = own_input.astype(F32) + dot(set_attended.astype(BF16), wso[...])
    set_out[...] = states[:cells].astype(BF16)


def on_device(
    n, m, gene_tokens, latents, head_temp, w_key, w_value, w_out, w_set_qkv, w_set_out, set_ids
):
    cells, genes, width = gene_tokens.shape
    rows = latents.shape[0]
    portion = rows // n
    hbm = pl.BlockSpec(memory_space=pltpu.HBM)
    vmem = pl.BlockSpec(memory_space=pltpu.VMEM)
    return tuple(
        pl.pallas_call(
            functools.partial(kernel, n, m),
            out_shape=(
                pltpu.VMEM((cells, portion, width), BF16),
                pltpu.VMEM((cells, width), BF16),
            ),
            in_specs=[hbm] * 9,
            out_specs=(vmem, vmem),
            scratch_shapes=[
                pltpu.VMEM(gene_tokens.shape, BF16),
                pltpu.VMEM(latents.shape, BF16),
                pltpu.VMEM(w_key.shape, BF16),
                pltpu.VMEM(w_value.shape, BF16),
                pltpu.VMEM(w_out.shape, BF16),
                pltpu.VMEM(w_set_qkv.shape, BF16),
                pltpu.VMEM(w_set_out.shape, BF16),
                pltpu.VMEM((width // GROUP, GROUP, GROUP), BF16),
                pltpu.VMEM((cells, n, portion, width), BF16),
                pltpu.VMEM((cells, n, portion, width), BF16),
                pltpu.VMEM((cells * portion, width), F32),
                pltpu.VMEM((ROWS, width // 2), F32),
                pltpu.VMEM((ROWS, width // 2), BF16),
                pltpu.VMEM((n, ROWS, width // 2), BF16),
                pltpu.VMEM((ROWS, width // 2), BF16),
                pltpu.VMEM((m, ROWS, width // 2), BF16),
                pltpu.VMEM((n, portion, LANES), BF16),
                pltpu.VMEM((n, portion, LANES), BF16),
                pltpu.VMEM((ROWS, LANES), F32),
                pltpu.VMEM((m, ROWS, LANES), F32),
                pltpu.VMEM((cells * portion, LANES), F32),
                pltpu.SMEM(head_temp.shape, F32),
                pltpu.SMEM(set_ids.shape, jnp.int32),
                pltpu.SemaphoreType.DMA((8,)),
                pltpu.SemaphoreType.DMA((cells,)),
                pltpu.SemaphoreType.DMA((cells,)),
                pltpu.SemaphoreType.DMA((cells,)),
                pltpu.SemaphoreType.DMA((8,)),
            ],
            compiler_params=pltpu.CompilerParams(
                collective_id=0, has_side_effects=True, vmem_limit_bytes=VMEM_BYTES
            ),
            name="latent_cross_attention",
        )(gene_tokens, latents, head_temp, w_key, w_value, w_out, w_set_qkv, w_set_out, set_ids)
    )


def solution(mesh):
    n, m = mesh.shape["gene"], mesh.shape["cell"]
    in_specs = (P("cell", "gene", None), P(), P(), P(), P(), P(), P(), P(), P("cell"))
    out_specs = (P("cell", "gene", None), P("cell", None))
    return jax.shard_map(
        functools.partial(on_device, n, m),
        mesh=mesh,
        in_specs=in_specs,
        out_specs=out_specs,
        check_vma=False,
    )
```
